256 devices in a mesh: row: 8 (over x, z_hi), col: 32 (over z_lo, y, core).
Axes of the slice: x: 4, y: 4, z: 8 (z_hi: 2, z_lo: 4; z = z_hi * 4 + z_lo), core: 2. Of those that a mesh axis runs over, the one named last changes fastest.
Arguments:
- adj_tiles: bfloat16 [8, 32, 160, 128, 128], P('row', 'col'), may hold values from -0.125 to 0.125
- tile_row: int32 [8, 32, 160], P('row', 'col'), may hold values from 0 to 31, as said below
- tile_col: int32 [8, 32, 160], P('row', 'col'), may hold values from 0 to 7
- tile_count: int32 [8, 32], P('row', 'col'), may hold values from 0 to 160, as said below
- node_feats: bfloat16 [32768, 512], P(('row', 'col')), may hold values from -24 to 24
- pre_act: bfloat16 [32768, 512], P(('col', 'row')), may hold values from -24 to 24
- out_grad: bfloat16 [32768, 512], P(('row', 'col')), may hold values from -0.08984375 to 0.08984375
- second_weight: bfloat16 [512, 512], replicated, may hold values from -0.25 to 0.25
Outputs:
- grad_first: float32 [512, 512], replicated
- grad_second: float32 [512, 512], replicated
The draws below stay inside these ranges and needn't reach their ends.
Inputs may be any that keep to these rules, and one draw needn't show every extreme that they name: Within one block the slots name distinct tile positions (tile_row, tile_col). `tile_count`: blocks whose node columns meet their node rows hold 80 to 160 live slots, one of them exactly 160; every other block holds at most 8.
All inputs are finite; a program needn't handle non-finite values.
Results may differ from the reference program's by a relative error of at most 0.024.
Values may be sent and summed in bfloat16 or wider, within the bound.
A program may use at most 128 MiB of HBM per device.

```python
import jax
import jax.numpy as jnp
from jax import lax

HIDDEN_SIZE = 512
FEATS = 512
TILE = 128
NODES = 32768
ROW_SPAN = 4096
COL_SPAN = 1024
ROW_TILES = 32
COL_TILES = 8
SLOTS = 160
N_ROW = 8
N_COL = 32


def tile_places(key):
    base_key = jax.random.fold_in(key, 11)
    device_keys = jax.random.split(base_key, N_ROW * N_COL)

    def one_device(device_key):
        return jax.random.permutation(device_key, ROW_TILES * COL_TILES)[:SLOTS]
    placed = jax.vmap(one_device)(device_keys)
    return placed.reshape(N_ROW, N_COL, SLOTS).astype(jnp.int32)


def draw_tile_row(key, part):
    return (tile_places(key) // COL_TILES).astype(jnp.int32)


def draw_tile_col(key, part):
    return (tile_places(key) % COL_TILES).astype(jnp.int32)


def draw_tile_count(key, part):
    base_key = jax.random.fold_in(key, 23)
    dense_key, sparse_key, chosen_key = jax.random.split(base_key, 3)
    grid_rows = jnp.arange(N_ROW, dtype=jnp.int32)[:, None]
    grid_cols = jnp.arange(N_COL, dtype=jnp.int32)[None, :]
    near = (grid_cols * COL_SPAN < (grid_rows + 1) * ROW_SPAN) & ((grid_cols + 1) * COL_SPAN > grid_rows * ROW_SPAN)
    dense = jax.random.randint(dense_key, (N_ROW, N_COL), SLOTS // 2, SLOTS + 1)
    sparse = jax.random.randint(sparse_key, (N_ROW, N_COL), 0, min(8, SLOTS) + 1)
    counts = jnp.where(near, dense, sparse)
    chosen_row = jax.random.randint(chosen_key, (), 0, N_ROW)
    chosen_col = chosen_row * ROW_SPAN // COL_SPAN
    counts = jnp.where((grid_rows == chosen_row) & (grid_cols == chosen_col), SLOTS, counts)
    return counts.astype(jnp.int32)


def with_spikes(result, own_key, source, target, parts, factor):
    def block_of(dim):
        return (jnp.arange(result.shape[dim]) // (result.shape[dim] // parts)).reshape((-1,) + (1,) * (result.ndim - 1 - dim))

    one_side = jax.random.permutation(own_key, parts)[block_of(target)]
    far = (block_of(target) + parts // 2) % parts
    return jnp.where((block_of(source) == one_side) | (block_of(source) == far), factor * result, result)


def level_of(own_key, dims, shards, smallest, top_value):
    level, own = 1.0, jax.random.fold_in(own_key, 6)
    for dim, parts in shards:
        heights = jnp.exp(jax.random.uniform(jax.random.fold_in(own, dim), (parts,), jnp.float32, smallest / len(shards), top_value / len(shards)))
        level = level * jnp.repeat(heights, dims[dim] // parts).reshape([-1 if axis == dim else 1 for axis in range(len(dims))])
    return level


def scatter_about(own_key, shape, deviation, most, cuts=(), kind=jnp.bfloat16):
    result = deviation * jax.random.normal(own_key, shape, jnp.float32)
    if cuts:
        result = result * level_of(own_key, shape, cuts, -0.22, 0.18)
    return jnp.clip(result, -most, most).astype(kind)


def bell_draw_with(stream_key, dims, width, most, cuts, heavy, kind=jnp.bfloat16):
    drawn = width * jax.random.normal(stream_key, dims, jnp.float32)
    if cuts:
        drawn = drawn * level_of(stream_key, dims, cuts, -0.22, 0.18)
    return jnp.clip(with_spikes(drawn, jax.random.fold_in(stream_key, 3), *heavy), -most, most).astype(kind)


def setup_inputs(seed: int = 0) -> dict:
    arg_keys = jax.random.split(jax.random.key(seed), 9)
    adj_tiles = scatter_about(arg_keys[0], (N_ROW, N_COL, SLOTS, TILE, TILE), (TILE * ROW_TILES // 2) ** -0.5, 0.125, ((0, 8), (1, 32)))
    tile_row = draw_tile_row(jax.random.fold_in(arg_keys[8], 71), 0)
    tile_col = draw_tile_col(jax.random.fold_in(arg_keys[8], 71), 0)
    tile_count = draw_tile_count(jax.random.fold_in(arg_keys[8], 71), 0)
    node_feats = bell_draw_with(arg_keys[4], (NODES, FEATS), 1.0, 24.0, ((0, 256),), (0, 1, 256, 6.0))
    pre_act = bell_draw_with(arg_keys[5], (NODES, HIDDEN_SIZE), 1.0, 24.0, ((0, 256),), (0, 1, 256, 6.0))
    out_grad = scatter_about(arg_keys[6], (NODES, HIDDEN_SIZE), 0.015, 0.08984375, ((0, 256),))
    second_weight = scatter_about(arg_keys[7], (HIDDEN_SIZE, HIDDEN_SIZE), HIDDEN_SIZE ** -0.5, 0.25)
    return {"adj_tiles": adj_tiles, "tile_row": tile_row, "tile_col": tile_col, "tile_count": tile_count, "node_feats": node_feats, "pre_act": pre_act, "out_grad": out_grad, "second_weight": second_weight}


def device_terms(local_tiles, in_index, out_index, live_count, panel, out_tiles, transpose):
    tile_size = local_tiles.shape[1]
    panel_width = panel.shape[1]
    blocked = panel.reshape(-1, tile_size, panel_width)
    gathered = blocked[in_index]
    if transpose:
        products = jnp.einsum("bij,biw->bjw", local_tiles.astype(jnp.float32), gathered.astype(jnp.float32))
    else:
        products = jnp.einsum("bij,bjw->biw", local_tiles.astype(jnp.float32), gathered.astype(jnp.float32))
    present = (jnp.arange(local_tiles.shape[0], dtype=jnp.int32) < live_count).astype(jnp.float32)
    select = (out_index[None, :] == jnp.arange(out_tiles, dtype=jnp.int32)[:, None]).astype(jnp.float32)
    select = select * present[None, :]
    summed = jnp.einsum("ob,bjw->ojw", select, products)
    return summed.reshape(out_tiles * tile_size, panel_width)


def spread_sum(adj_tiles, tile_row, tile_col, tile_count, panel, transpose):
    grid_tiles = adj_tiles.reshape(N_ROW * N_COL, SLOTS, TILE, TILE)
    rows_flat = tile_row.reshape(N_ROW * N_COL, SLOTS)
    cols_flat = tile_col.reshape(N_ROW * N_COL, SLOTS)
    counts_flat = tile_count.reshape(N_ROW * N_COL)
    panel_width = panel.shape[1]
    initial = jnp.zeros((NODES, panel_width), jnp.float32)

    def visit_device(device, running):
        device = jnp.asarray(device).astype(jnp.int32)
        grid_row = device // N_COL
        grid_col = device % N_COL
        if transpose:
            source = lax.dynamic_slice_in_dim(panel, (grid_row * ROW_SPAN).astype(jnp.int32), ROW_SPAN, 0)
            contrib = device_terms(grid_tiles[device], rows_flat[device], cols_flat[device], counts_flat[device], source, COL_TILES, True)
            target_start = (grid_col * COL_SPAN).astype(jnp.int32)
            target_len = COL_SPAN
        else:
            source = lax.dynamic_slice_in_dim(panel, (grid_col * COL_SPAN).astype(jnp.int32), COL_SPAN, 0)
            contrib = device_terms(grid_tiles[device], cols_flat[device], rows_flat[device], counts_flat[device], source, ROW_TILES, False)
            target_start = (grid_row * ROW_SPAN).astype(jnp.int32)
            target_len = ROW_SPAN
        current = lax.dynamic_slice_in_dim(running, target_start, target_len, 0)
        return lax.dynamic_update_slice_in_dim(running, current + contrib, target_start, 0)

    return lax.fori_loop(0, N_ROW * N_COL, visit_device, initial)


def reference(adj_tiles, tile_row, tile_col, tile_count, node_feats, pre_act, out_grad, second_weight):
    hidden_act = jnp.maximum(pre_act, 0)
    back_agg = spread_sum(adj_tiles, tile_row, tile_col, tile_count, out_grad, True).astype(jnp.bfloat16)
    grad_second = lax.dot_general(hidden_act, back_agg, (((0,), (0,)), ((), ())), preferred_element_type=jnp.float32)
    hidden_grad = lax.dot_general(back_agg, second_weight, (((1,), (1,)), ((), ())), preferred_element_type=jnp.float32)
    pre_grad = jnp.where(pre_act > 0, hidden_grad, 0.0).astype(jnp.bfloat16)
    fwd_agg = spread_sum(adj_tiles, tile_row, tile_col, tile_count, pre_grad, False).astype(jnp.bfloat16)
    grad_first = lax.dot_general(node_feats, fwd_agg, (((0,), (0,)), ((), ())), preferred_element_type=jnp.float32)
    return grad_first, grad_second
```

```python
import functools

import jax
import jax.numpy as jnp
from jax import lax
from jax.experimental import pallas as pl
from jax.experimental.pallas import tpu as pltpu
from jax.sharding import PartitionSpec as P

MESH = pl.DeviceIdType.MESH
BF16 = jnp.bfloat16
F32 = jnp.float32
NX, NY, NZL, NZH = 4, 4, 4, 2
NT = (((1,), (1,)), ((), ()))


def whole_kernel(
    inv,
    tiles_hbm,
    feats,
    pre,
    cot,
    weight,
    out,
    tiles,
    gathered,
    acc,
    part,
    from_x,
    to_z,
    from_z,
    pre_t,
    grad_t,
    own,
    sent,
    core_in,
    half,
    plane_in,
    z_in,
    final,
    tile_sem,
    ag_send,
    ag_recv,
    rx_send,
    rx_recv,
    rz_send,
    rz_recv,
    core_send,
    core_recv,
    plane_send,
    plane_recv,
    z_send,
    z_recv,
    fin_send,
    fin_recv,
    last_send,
    last_recv,
):
    r = lax.axis_index("row")
    c = lax.axis_index("col")
    x, zh = r // NZH, r % NZH
    zl, y, k = c // (2 * NY), (c // 2) % NY, c % 2
    z = zh * NZL + zl
    live_slots = tiles_hbm.shape[0]

    def device(x_, zh_, zl_, y_, k_):
        return (x_ * NZH + zh_, (zl_ * NY + y_) * 2 + k_)

    def slot(zl_, y_, k_):
        return (zl_ * NY + y_) * 2 + k_

    sibling = device(x, zh, zl, y, 1 - k)
    y_up = device(x, zh, zl, (y + 1) % NY, k)
    y_down = device(x, zh, zl, (y + NY - 1) % NY, k)
    plane = []
    for dx in range(NX):
        for dy in range(NY):
            if dx or dy:
                xx, yy = (x + dx) % NX, (y + dy) % NY
                plane.append((xx * NY + yy, device(xx, zh, zl, yy, k)))
    z_line = []
    for dz in range(1, NZH * NZL):
        zz = (z + dz) % (NZH * NZL)
        z_line.append((zz, device(x, zz // NZL, zz % NZL, y, k)))

    def send(src, dst, ssem, rsem, dev):
        copy = pltpu.make_async_remote_copy(
            src_ref=src, dst_ref=dst, send_sem=ssem, recv_sem=rsem, device_id=dev, device_id_type=MESH
        )
        copy.start()
        return copy

    def arrived(ref, ssem, rsem):
        pltpu.make_async_remote_copy(
            src_ref=ref, dst_ref=ref, send_sem=ssem, recv_sem=rsem, device_id=sibling, device_id_type=MESH
        ).wait_recv()

    load_tiles = pltpu.make_async_copy(tiles_hbm, tiles.at[pl.ds(0, live_slots)], tile_sem)
    load_tiles.start()

    barrier = pltpu.get_barrier_semaphore()
    greet = [sibling] + [d for _, d in plane] + [d for _, d in z_line]
    for dev in greet:
        pl.semaphore_signal(barrier, inc=1, device_id=dev, device_id_type=MESH)
    gathered[0, c] = cot[...].T
    gathered[1, c] = feats[...].T
    pre_t[...] = pre[...].T
    tiles[live_slots] = jnp.zeros(tiles.shape[1:], BF16)
    pl.semaphore_wait(barrier, len(greet))

    sends = []
    counts = [0, 0]

    def forward(w, s, dev):
        n = counts[w]
        counts[w] += 1
        ref = gathered.at[w, s]
        sends.append(send(ref, ref, ag_send.at[w, n], ag_recv.at[w, s], dev))

    def landed(w, s):
        arrived(gathered.at[w, s], ag_send.at[w, 0], ag_recv.at[w, s])

    def plane_of(d):
        return (zl + d) % NZL

    def own_rows(i):
        w, d = divmod(i, NZL)
        s = slot(plane_of(d), y, k)
        if d:
            landed(w, s)
        forward(w, s, y_up)
        forward(w, s, y_down)
        forward(w, s, sibling)

    def near_rows(i):
        w, d = divmod(i, NZL)
        below = slot(plane_of(d), (y + NY - 1) % NY, k)
        above = slot(plane_of(d), (y + 1) % NY, k)
        landed(w, below)
        if d < NZL // 2:
            forward(w, below, y_up)
        forward(w, below, sibling)
        landed(w, above)
        if d >= NZL // 2:
            forward(w, above, y_down)
        forward(w, above, sibling)

    def far_rows(i):
        w, d = divmod(i, NZL)
        far = slot(plane_of(d), (y + 2) % NY, k)
        landed(w, far)
        forward(w, far, sibling)

    def product(w, base, q):
        left = jnp.concatenate([gathered[w, base + j] for j in range(2 * NY)], axis=1)
        right = jnp.concatenate(
            [
                jnp.concatenate([tiles[inv[(base + j) * 8 + 2 * q + h]] for h in range(2)], axis=1)
                for j in range(2 * NY)
            ],
            axis=0,
        )
        return jnp.dot(left, right, preferred_element_type=F32)

    def multiply(i):
        w, d = divmod(i, NZL)
        for yy in range(NY):
            landed(w, slot(plane_of(d), yy, 1 - k))
        base = slot(plane_of(d), 0, 0)
        if d < NZL - 1:

            def one(q, carry):
                value = product(w, base, q)
                acc[w, q] = value if d == 0 else acc[w, q] + value
                return carry

            lax.fori_loop(0, NX, one, 0)
            return
        for j in range(NX):
            q = (x + 1 + j) % NX
            value = acc[w, q] + product(w, base, q)
            if j < NX - 1:
                part[w, j] = value.astype(BF16)
                dev = device(q, zh, zl, y, k)
                sends.append(send(part.at[w, j], from_x.at[w, j], rx_send.at[w, j], rx_recv.at[w, j], dev))
            else:
                acc[w, q] = value

    def x_sum(w, which):
        lanes = pl.ds(pl.multiple_of(which * 128, 128), 128)
        total = acc[w, x, :, lanes]
        for j in range(NX - 1):
            total = total + from_x[w, j, :, lanes].astype(F32)
        return total

    def over_x(w):
        for j in range(NX - 1):
            arrived(from_x.at[w, j], rx_send.at[w, j], rx_recv.at[w, j])
        to_z[w] = x_sum(w, 1 - zh).astype(BF16)
        sends.append(send(to_z.at[w], from_z.at[w], rz_send.at[w], rz_recv.at[w], device(x, 1 - zh, zl, y, k)))

    def over_z(w):
        kept = x_sum(w, zh)
        arrived(from_z.at[w], rz_send.at[w], rz_recv.at[w])
        return (kept + from_z[w].astype(F32)).astype(BF16)

    def local(w):
        agg = over_z(w)
        if w == 0:
            left = jnp.maximum(pre_t[...], jnp.zeros((), BF16))
            grad = lax.dot_general(left, agg, NT, preferred_element_type=F32)
        else:
            grad = lax.dot_general(agg, grad_t[...], NT, preferred_element_type=F32)
        own[w] = grad
        sent[w] = grad.astype(BF16)
        rows = pl.ds(pl.multiple_of((1 - k) * 256, 256), 256)
        sends.append(send(sent.at[w, rows], core_in.at[w], core_send.at[w], core_recv.at[w], sibling))
        if w == 0:
            hidden = jnp.dot(weight[...], agg, preferred_element_type=F32)
            grad_t[...] = jnp.where(pre_t[...] > 0, hidden, 0.0).astype(BF16)

    me = x * NY + y

    def core_sum(w):
        arrived(core_in.at[w], core_send.at[w], core_recv.at[w])
        rows = pl.ds(pl.multiple_of(k * 256, 256), 256)
        total = own[w, rows] + core_in[w].astype(F32)
        half[w] = total.astype(BF16).reshape(NX * NY, 16, 512)
        for m, dev in plane:
            sends.append(
                send(half.at[w, m], plane_in.at[w, me], plane_send.at[w, m], plane_recv.at[w, me], dev)
            )

    def plane_sum(w):
        total = half[w, me].astype(F32)
        for m, _ in plane:
            arrived(plane_in.at[w, m], plane_send.at[w, m], plane_recv.at[w, m])
            total = total + plane_in[w, m].astype(F32)
        z_in[w, z] = total.astype(BF16)
        for zz, dev in z_line:
            sends.append(send(z_in.at[w, z], z_in.at[w, z], z_send.at[w, zz], z_recv.at[w, z], dev))

    def z_sum(w):
        for zz, _ in z_line:
            arrived(z_in.at[w, zz], z_send.at[w, zz], z_recv.at[w, zz])
        total = z_in[w, 0].astype(F32)
        for zz in range(1, NZH * NZL):
            total = total + z_in[w, zz].astype(F32)
        final[w, k, me] = total.astype(BF16)
        for m, dev in plane:
            ref = final.at[w, k, me]
            sends.append(send(ref, ref, fin_send.at[w, m], fin_recv.at[w, me], dev))

    def share(w):
        for m, _ in plane:
            arrived(final.at[w, k, m], fin_send.at[w, m], fin_recv.at[w, m])
        ref = final.at[w, k]
        sends.append(send(ref, ref, last_send.at[w], last_recv.at[w], sibling))

    def finish(w):
        arrived(final.at[w, 1 - k], last_send.at[w], last_recv.at[w])
        out[w] = final[w].reshape(512, 512)

    for w in range(2):
        for d in range(1, NZL):
            forward(w, c, device(x, zh, (zl + d) % NZL, y, k))
    load_tiles.wait()

    steps = 2 * NZL
    for i in range(steps + 3):
        if i < steps:
            own_rows(i)
        if 0 <= i - 1 < steps:
            near_rows(i - 1)
        if 0 <= i - 2 < steps:
            far_rows(i - 2)
        if 0 <= i - 3 < steps:
            multiply(i - 3)
        if i == NZL + 4:
            over_x(0)
        if i == NZL + 5:
            local(0)
    core_sum(0)
    over_x(1)
    plane_sum(0)
    local(1)
    core_sum(1)
    z_sum(0)
    plane_sum(1)
    share(0)
    z_sum(1)
    finish(0)
    share(1)
    finish(1)
    for copy in sends:
        copy.wait_send()


def shards(adj_tiles, tile_row, tile_col, tile_count, node_feats, pre_act, out_grad, second_weight):
    tiles = adj_tiles[0, 0]
    slots = tiles.shape[0]
    live = jnp.arange(slots, dtype=jnp.int32) < tile_count[0, 0]
    place = jnp.where(live, tile_row[0, 0] * 8 + tile_col[0, 0], -1)
    hit = place[None, :] == jnp.arange(256, dtype=jnp.int32)[:, None]
    inv = jnp.min(jnp.where(hit, jnp.arange(slots, dtype=jnp.int32)[None, :], slots), axis=1)
    vmem = pl.BlockSpec(memory_space=pltpu.VMEM)
    dma = pltpu.SemaphoreType.DMA
    result = pl.pallas_call(
        whole_kernel,
        out_shape=jax.ShapeDtypeStruct((2, 512, 512), BF16),
        in_specs=[pl.BlockSpec(memory_space=pltpu.SMEM), pl.BlockSpec(memory_space=pl.ANY)] + [vmem] * 4,
        out_specs=vmem,
        scratch_shapes=[
            pltpu.VMEM((slots + 1, 128, 128), BF16),
            pltpu.VMEM((2, 32, 512, 128), BF16),
            pltpu.VMEM((2, 4, 512, 256), F32),
            pltpu.VMEM((2, 3, 512, 256), BF16),
            pltpu.VMEM((2, 3, 512, 256), BF16),
            pltpu.VMEM((2, 512, 128), BF16),
            pltpu.VMEM((2, 512, 128), BF16),
            pltpu.VMEM((512, 128), BF16),
            pltpu.VMEM((512, 128), BF16),
            pltpu.VMEM((2, 512, 512), F32),
            pltpu.VMEM((2, 512, 512), BF16),
            pltpu.VMEM((2, 256, 512), BF16),
            pltpu.VMEM((2, 16, 16, 512), BF16),
            pltpu.VMEM((2, 16, 16, 512), BF16),
            pltpu.VMEM((2, 8, 16, 512), BF16),
            pltpu.VMEM((2, 2, 16, 16, 512), BF16),
            dma,
            dma((2, 31)),
            dma((2, 32)),
            dma((2, 3)),
            dma((2, 3)),
            dma((2,)),
            dma((2,)),
            dma((2,)),
            dma((2,)),
            dma((2, 16)),
            dma((2, 16)),
            dma((2, 8)),
            dma((2, 8)),
            dma((2, 16)),
            dma((2, 16)),
            dma((2,)),
            dma((2,)),
        ],
        compiler_params=pltpu.CompilerParams(
            collective_id=0, has_side_effects=True, vmem_limit_bytes=56 * 1024 * 1024
        ),
    )(inv, tiles, node_feats, pre_act, out_grad, second_weight)
    return result[1].astype(F32), result[0].astype(F32)


def solution(mesh):
    in_specs = (
        P("row", "col", None, None, None),
        P("row", "col", None),
        P("row", "col", None),
        P("row", "col"),
        P(("row", "col"), None),
        P(("col", "row"), None),
        P(("row", "col"), None),
        P(),
    )
    out_specs = (P(), P())
    return jax.shard_map(shards, mesh=mesh, in_specs=in_specs, out_specs=out_specs, check_vma=False)
```

```python
import functools

import jax
import jax.numpy as jnp
from jax import lax
from jax.experimental import pallas as pl
from jax.experimental.pallas import tpu as pltpu
from jax.sharding import PartitionSpec as P

MESH = pl.DeviceIdType.MESH
BF16 = jnp.bfloat16
F32 = jnp.float32
NX, NY, NZL, NZH = 4, 4, 4, 2
CHUNKS = 4
HALF = 256
UNIT_ROWS = (512, 256, 256)
UNIT_START = (0, 512, 768)
NT = (((1,), (1,)), ((), ()))


def whole_kernel(inv, tiles_hbm, feats, pre, cot, weight, out, *scratch):
    (tiles, gathered, acc, part, from_x, to_z, from_z, agg, pre_t, grad_t, z_in0, z_in1, z_in2) = scratch[:13]
    z_in = (z_in0, z_in1, z_in2)
    kept, given, core_in, piece, plane_in, final = (scratch[13 + 3 * n : 16 + 3 * n] for n in range(6))
    (tile_sem, ag_send, ag_recv, rx_send, rx_recv, rz_send, rz_recv) = scratch[31:38]
    (core_send, core_recv, plane_send, plane_recv, z_send, z_recv) = scratch[38:44]
    (fin_send, fin_recv, last_send, last_recv) = scratch[44:]
    r = lax.axis_index("row")
    c = lax.axis_index("col")
    x, zh = r // NZH, r % NZH
    zl, y, k = c // (2 * NY), (c // 2) % NY, c % 2
    z = zh * NZL + zl
    live_slots = tiles_hbm.shape[0]

    def device(x_, zh_, zl_, y_, k_):
        return (x_ * NZH + zh_, (zl_ * NY + y_) * 2 + k_)

    def slot(zl_, y_, k_):
        return (zl_ * NY + y_) * 2 + k_

    sibling = device(x, zh, zl, y, 1 - k)
    y_up = device(x, zh, zl, (y + 1) % NY, k)
    y_down = device(x, zh, zl, (y + NY - 1) % NY, k)
    plane = []
    for dx in range(NX):
        for dy in range(NY):
            if dx or dy:
                xx, yy = (x + dx) % NX, (y + dy) % NY
                plane.append((xx * NY + yy, device(xx, zh, zl, yy, k)))
    z_line = []
    for dz in range(1, NZH * NZL):
        zz = (z + dz) % (NZH * NZL)
        z_line.append((zz, device(x, zz // NZL, zz % NZL, y, k)))
    me = x * NY + y

    sends = []

    def send(src, dst, ssem, rsem, dev):
        copy = pltpu.make_async_remote_copy(
            src_ref=src, dst_ref=dst, send_sem=ssem, recv_sem=rsem, device_id=dev, device_id_type=MESH
        )
        copy.start()
        sends.append(copy)

    def arrived(ref, ssem, rsem):
        pltpu.make_async_remote_copy(
            src_ref=ref, dst_ref=ref, send_sem=ssem, recv_sem=rsem, device_id=sibling, device_id_type=MESH
        ).wait_recv()

    load_tiles = pltpu.make_async_copy(tiles_hbm, tiles.at[pl.ds(0, live_slots)], tile_sem)
    load_tiles.start()

    barrier = pltpu.get_barrier_semaphore()
    greet = [sibling] + [d for _, d in plane] + [d for _, d in z_line]
    for dev in greet:
        pl.semaphore_signal(barrier, inc=1, device_id=dev, device_id_type=MESH)
    for w, source in enumerate((cot, feats)):
        turned = source[...].T
        gathered[2 * w, c] = turned[:HALF]
        gathered[2 * w + 1, c] = turned[HALF:]
    pre_t[...] = pre[...].T
    tiles[live_slots] = jnp.zeros(tiles.shape[1:], BF16)
    pl.semaphore_wait(barrier, len(greet))

    counts = [0] * CHUNKS

    def forward(ch, s, dev):
        n = counts[ch]
        counts[ch] += 1
        ref = gathered.at[ch, s]
        send(ref, ref, ag_send.at[ch, n], ag_recv.at[ch, s], dev)

    def landed(ch, s):
        arrived(gathered.at[ch, s], ag_send.at[ch, 0], ag_recv.at[ch, s])

    def plane_of(d):
        return (zl + d) % NZL

    def spread(ch, s):
        forward(ch, s, y_up)
        forward(ch, s, y_down)
        forward(ch, s, sibling)

    def own_rows(ch, d):
        if d:
            s = slot(plane_of(d), y, k)
            landed(ch, s)
            spread(ch, s)

    def near_rows(ch, d):
        turn = (k + d) % 2
        first = slot(plane_of(d), (y + NY - 1 + 2 * turn) % NY, k)
        second = slot(plane_of(d), (y + 1 + 2 * turn) % NY, k)
        landed(ch, first)
        forward(ch, first, device(x, zh, zl, (y + 1 + 2 * turn) % NY, k))
        forward(ch, first, sibling)
        landed(ch, second)
        forward(ch, second, sibling)

    def far_rows(ch, d):
        far = slot(plane_of(d), (y + 2) % NY, k)
        landed(ch, far)
        forward(ch, far, sibling)

    def product(ch, base, q):
        left = jnp.concatenate([gathered[ch, base + j] for j in range(2 * NY)], axis=1)
        right = jnp.concatenate(
            [
                jnp.concatenate([tiles[inv[(base + j) * 8 + 2 * q + h]] for h in range(2)], axis=1)
                for j in range(2 * NY)
            ],
            axis=0,
        )
        return jnp.dot(left, right, preferred_element_type=F32)

    def multiply(ch, d):
        for yy in range(NY):
            landed(ch, slot(plane_of(d), yy, 1 - k))
        base = slot(plane_of(d), 0, 0)
        if d < NZL - 1:

            def one(q, carry):
                value = product(ch, base, q)
                acc[ch, q] = value if d == 0 else acc[ch, q] + value
                return carry

            lax.fori_loop(0, NX, one, 0)
            return
        for j in range(NX):
            q = (x + 1 + j) % NX
            value = acc[ch, q] + product(ch, base, q)
            if j < NX - 1:
                part[ch, j] = value.astype(BF16)
                dev = device(q, zh, zl, y, k)
                send(part.at[ch, j], from_x.at[ch, j], rx_send.at[ch, j], rx_recv.at[ch, j], dev)
            else:
                acc[ch, q] = value

    def x_sum(ch, which):
        lanes = pl.ds(pl.multiple_of(which * 128, 128), 128)
        total = acc[ch, x, :, lanes]
        for j in range(NX - 1):
            total = total + from_x[ch, j, :, lanes].astype(F32)
        return total

    def over_x(ch):
        for j in range(NX - 1):
            arrived(from_x.at[ch, j], rx_send.at[ch, j], rx_recv.at[ch, j])
        to_z[ch] = x_sum(ch, 1 - zh).astype(BF16)
        send(to_z.at[ch], from_z.at[ch], rz_send.at[ch], rz_recv.at[ch], device(x, 1 - zh, zl, y, k))

    def over_z(ch):
        total = x_sum(ch, zh)
        arrived(from_z.at[ch], rz_send.at[ch], rz_recv.at[ch])
        rows = pl.ds((ch % 2) * HALF, HALF)
        agg[ch // 2, rows] = (total + from_z[ch].astype(F32)).astype(BF16)

    def local(u):
        rows = UNIT_ROWS[u] // 2

        def share_of(core):
            start = pl.multiple_of(core * rows, rows)
            if u == 0:
                left = jnp.maximum(pre_t[pl.ds(start, rows)], jnp.zeros((), BF16))
                right = agg[0]
            else:
                left = agg[1, pl.ds((u - 1) * HALF + start, rows)]
                right = grad_t[...]
            return lax.dot_general(left, right, NT, preferred_element_type=F32)

        given[u][...] = share_of(1 - k).astype(BF16)
        send(given[u], core_in[u], core_send.at[u], core_recv.at[u], sibling)
        kept[u][...] = share_of(k)
        if u == 0:
            hidden = jnp.dot(weight[...], agg[0], preferred_element_type=F32)
            grad_t[...] = jnp.where(pre_t[...] > 0, hidden, 0.0).astype(BF16)

    def core_sum(u):
        arrived(core_in[u], core_send.at[u], core_recv.at[u])
        total = (kept[u][...] + core_in[u][...].astype(F32)).astype(BF16)
        wide = UNIT_ROWS[u]
        cuts = 512 // wide
        for m in range(NX * NY):
            top, left = (m // cuts) * 16, (m % cuts) * wide
            piece[u][m] = total[top : top + 16, left : left + wide]
        for m, dev in plane:
            send(piece[u].at[m], plane_in[u].at[me], plane_send.at[u, m], plane_recv.at[u, me], dev)

    def plane_sum(u):
        total = piece[u][me].astype(F32)
        for m, _ in plane:
            arrived(plane_in[u].at[m], plane_send.at[u, m], plane_recv.at[u, m])
            total = total + plane_in[u][m].astype(F32)
        z_in[u][z] = total.astype(BF16)
        for zz, dev in z_line:
            send(z_in[u].at[z], z_in[u].at[z], z_send.at[u, zz], z_recv.at[u, z], dev)

    def z_sum(u):
        for zz, _ in z_line:
            arrived(z_in[u].at[zz], z_send.at[u, zz], z_recv.at[u, zz])
        total = z_in[u][0].astype(F32)
        for zz in range(1, NZH * NZL):
            total = total + z_in[u][zz].astype(F32)
        final[u][k, me] = total.astype(BF16)
        ref = final[u].at[k, me]
        for m, dev in plane:
            send(ref, ref, fin_send.at[u, m], fin_recv.at[u, me], dev)

    def share(u):
        for m, _ in plane:
            arrived(final[u].at[k, m], fin_send.at[u, m], fin_recv.at[u, m])
        ref = final[u].at[k]
        send(ref, ref, last_send.at[u], last_recv.at[u], sibling)

    def finish(u):
        arrived(final[u].at[1 - k], last_send.at[u], last_recv.at[u])
        wide = UNIT_ROWS[u]
        cuts = 512 // wide
        base = UNIT_START[u]
        for core in range(2):
            for m in range(NX * NY):
                top, left = base + core * (wide // 2) + (m // cuts) * 16, (m % cuts) * wide
                out[top : top + 16, left : left + wide] = final[u][core, m]

    for ch in range(CHUNKS):
        for d in range(NZL - 1, 0, -1):
            forward(ch, c, device(x, zh, (zl + d) % NZL, y, k))
    for ch in range(CHUNKS):
        spread(ch, c)
    load_tiles.wait()

    steps = [(ch, d) for ch in range(CHUNKS) for d in range(NZL)]
    for i in range(len(steps) + 7):
        for lag, job in ((0, own_rows), (3, near_rows), (6, far_rows)):
            if 0 <= i - lag < len(steps):
                job(*steps[i - lag])
        if i >= 14 and (i - 14) % NZL == 0 and (i - 14) // NZL < CHUNKS:
            over_x((i - 14) // NZL)
        if i == 17:
            over_z(0)
        if i == 21:
            over_z(1)
            local(0)
        if i >= 7:
            multiply(*steps[i - 7])
    core_sum(0)
    over_z(2)
    local(1)
    core_sum(1)
    over_x(3)
    plane_sum(0)
    plane_sum(1)
    over_z(3)
    local(2)
    z_sum(0)
    core_sum(2)
    z_sum(1)
    share(0)
    plane_sum(2)
    share(1)
    finish(0)
    z_sum(2)
    finish(1)
    share(2)
    finish(2)
    for copy in sends:
        copy.wait_send()


def shards(adj_tiles, tile_row, tile_col, tile_count, node_feats, pre_act, out_grad, second_weight):
    tiles = adj_tiles[0, 0]
    slots = tiles.shape[0]
    live = jnp.arange(slots, dtype=jnp.int32) < tile_count[0, 0]
    place = jnp.where(live, tile_row[0, 0] * 8 + tile_col[0, 0], -1)
    hit = place[None, :] == jnp.arange(256, dtype=jnp.int32)[:, None]
    inv = jnp.min(jnp.where(hit, jnp.arange(slots, dtype=jnp.int32)[None, :], slots), axis=1)
    vmem = pl.BlockSpec(memory_space=pltpu.VMEM)
    dma = pltpu.SemaphoreType.DMA
    result = pl.pallas_call(
        whole_kernel,
        out_shape=jax.ShapeDtypeStruct((1024, 512), BF16),
        in_specs=[pl.BlockSpec(memory_space=pltpu.SMEM), pl.BlockSpec(memory_space=pl.ANY)] + [vmem] * 4,
        out_specs=vmem,
        scratch_shapes=[
            pltpu.VMEM((slots + 1, 128, 128), BF16),
            pltpu.VMEM((CHUNKS, 32, HALF, 128), BF16),
            pltpu.VMEM((CHUNKS, NX, HALF, 256), F32),
            pltpu.VMEM((CHUNKS, 3, HALF, 256), BF16),
            pltpu.VMEM((CHUNKS, 3, HALF, 256), BF16),
            pltpu.VMEM((CHUNKS, HALF, 128), BF16),
            pltpu.VMEM((CHUNKS, HALF, 128), BF16),
            pltpu.VMEM((2, 512, 128), BF16),
            pltpu.VMEM((512, 128), BF16),
            pltpu.VMEM((512, 128), BF16),
        ]
        + [pltpu.VMEM((8, 16, n), BF16) for n in UNIT_ROWS]
        + [pltpu.VMEM((n // 2, 512), F32) for n in UNIT_ROWS]
        + [pltpu.VMEM((n // 2, 512), BF16) for n in UNIT_ROWS]
        + [pltpu.VMEM((n // 2, 512), BF16) for n in UNIT_ROWS]
        + [pltpu.VMEM((16, 16, n), BF16) for n in UNIT_ROWS]
        + [pltpu.VMEM((16, 16, n), BF16) for n in UNIT_ROWS]
        + [pltpu.VMEM((2, 16, 16, n), BF16) for n in UNIT_ROWS]
        + [
            dma,
            dma((CHUNKS, 31)),
            dma((CHUNKS, 32)),
            dma((CHUNKS, 3)),
            dma((CHUNKS, 3)),
            dma((CHUNKS,)),
            dma((CHUNKS,)),
            dma((3,)),
            dma((3,)),
            dma((3, 16)),
            dma((3, 16)),
            dma((3, 8)),
            dma((3, 8)),
            dma((3, 16)),
            dma((3, 16)),
            dma((3,)),
            dma((3,)),
        ],
        compiler_params=pltpu.CompilerParams(
            collective_id=0, has_side_effects=True, vmem_limit_bytes=56 * 1024 * 1024
        ),
    )(inv, tiles, node_feats, pre_act, out_grad, second_weight)
    return result[512:].astype(F32), result[:512].astype(F32)


def solution(mesh):
    in_specs = (
        P("row", "col", None, None, None),
        P("row", "col", None),
        P("row", "col", None),
        P("row", "col"),
        P(("row", "col"), None),
        P(("col", "row"), None),
        P(("row", "col"), None),
        P(),
    )
    out_specs = (P(), P())
    return jax.shard_map(shards, mesh=mesh, in_specs=in_specs, out_specs=out_specs, check_vma=False)
```

```python
import functools

import jax
import jax.numpy as jnp
from jax import lax
from jax.experimental import pallas as pl
from jax.experimental.pallas import tpu as pltpu
from jax.sharding import PartitionSpec as P

MESH = pl.DeviceIdType.MESH
BF16 = jnp.bfloat16
F32 = jnp.float32
NX, NY, NZL, NZH = 4, 4, 4, 2
WIDTH = (256, 256, 256, 128, 128)
START = (0, 256, 0, 256, 384)
SIDE = (0, 0, 1, 1, 1)
CHUNKS = len(WIDTH)
UNIT_ROWS = (512, 256, 256)
UNIT_START = (0, 512, 768)
UNITS = len(UNIT_ROWS)
NT = (((1,), (1,)), ((), ()))


def whole_kernel(row_hbm, col_hbm, live, tiles_hbm, feats_hbm, pre_hbm, cot_hbm, weight_hbm, out, *scratch):
    scratch = list(scratch)

    def take(n=None):
        if n is None:
            return scratch.pop(0)
        return [scratch.pop(0) for _ in range(n)]

    tiles, feats, pre, cot, weight, places, table, inv = take(8)
    gathered, acc, part, from_x, to_z, from_z = (take(CHUNKS) for _ in range(6))
    agg, pre_t, grad_t = take(3)
    z_in, kept, given, core_in, piece, plane_in, final = (take(UNITS) for _ in range(7))
    tile_sem, load_sem, ag_send, ag_recv, rx_send, rx_recv, rz_send, rz_recv = take(8)
    core_send, core_recv, plane_send, plane_recv, z_send, z_recv = take(6)
    fin_send, fin_recv, last_send, last_recv = take(4)
    r = lax.axis_index("row")
    c = lax.axis_index("col")
    x, zh = r // NZH, r % NZH
    zl, y, k = c // (2 * NY), (c // 2) % NY, c % 2
    z = zh * NZL + zl
    live_slots = tiles_hbm.shape[0]

    def device(x_, zh_, zl_, y_, k_):
        return (x_ * NZH + zh_, (zl_ * NY + y_) * 2 + k_)

    def slot(zl_, y_, k_):
        return (zl_ * NY + y_) * 2 + k_

    sibling = device(x, zh, zl, y, 1 - k)
    y_up = device(x, zh, zl, (y + 1) % NY, k)
    y_down = device(x, zh, zl, (y + NY - 1) % NY, k)
    plane = []
    for dx in range(NX):
        for dy in range(NY):
            if dx or dy:
                xx, yy = (x + dx) % NX, (y + dy) % NY
                plane.append((xx * NY + yy, device(xx, zh, zl, yy, k)))
    z_line = []
    for dz in range(1, NZH * NZL):
        zz = (z + dz) % (NZH * NZL)
        z_line.append((zz, device(x, zz // NZL, zz % NZL, y, k)))
    me = x * NY + y

    sends = []

    def send(src, dst, ssem, rsem, dev):
        copy = pltpu.make_async_remote_copy(
            src_ref=src, dst_ref=dst, send_sem=ssem, recv_sem=rsem, device_id=dev, device_id_type=MESH
        )
        copy.start()
        sends.append(copy)

    def arrived(ref, ssem, rsem):
        pltpu.make_async_remote_copy(
            src_ref=ref, dst_ref=ref, send_sem=ssem, recv_sem=rsem, device_id=sibling, device_id_type=MESH
        ).wait_recv()

    load_tiles = pltpu.make_async_copy(tiles_hbm, tiles.at[pl.ds(0, live_slots)], tile_sem.at[0])
    loads = [
        pltpu.make_async_copy(src, dst, load_sem.at[n])
        for n, (src, dst) in enumerate(
            [
                (cot_hbm, cot),
                (feats_hbm, feats),
                (row_hbm, places.at[0]),
                (col_hbm, places.at[1]),
                (pre_hbm, pre),
                (weight_hbm, weight),
            ]
        )
    ]
    for copy in loads:
        copy.start()
    load_tiles.start()

    barrier = pltpu.get_barrier_semaphore()
    greet = [d for _, d in z_line] + [d for _, d in plane] + [sibling]
    for dev in greet:
        pl.semaphore_signal(barrier, inc=1, device_id=dev, device_id_type=MESH)
    for side, source in enumerate((cot, feats)):
        loads[side].wait()
        turned = source[...].T
        for ch in range(CHUNKS):
            if SIDE[ch] == side:
                gathered[ch][c] = turned[START[ch] : START[ch] + WIDTH[ch]]
    loads[2].wait()
    loads[3].wait()
    turn = lax.broadcasted_iota(jnp.int32, (1, live_slots), 1)
    place = jnp.where(turn < live[0, 0], places[0] * 8 + places[1], -1)
    hit = place == lax.broadcasted_iota(jnp.int32, (256, live_slots), 0)
    found = jnp.min(jnp.where(hit, turn, live_slots), axis=1, keepdims=True)
    table[...] = jnp.broadcast_to(found, (256, 128)).T[0:8]
    to_scalar = pltpu.make_async_copy(table, inv, tile_sem.at[1])
    to_scalar.start()
    tiles[live_slots] = jnp.zeros(tiles.shape[1:], BF16)
    loads[4].wait()
    pre_t[...] = pre[...].T
    loads[5].wait()
    to_scalar.wait()
    pl.semaphore_wait(barrier, len(greet))

    counts = [0] * CHUNKS

    def forward(ch, s, dev):
        n = counts[ch]
        counts[ch] += 1
        ref = gathered[ch].at[s]
        send(ref, ref, ag_send.at[ch, n], ag_recv.at[ch, s], dev)

    def landed(ch, s):
        arrived(gathered[ch].at[s], ag_send.at[ch, 0], ag_recv.at[ch, s])

    def plane_of(d):
        return (zl + d) % NZL

    def spread(ch, s):
        forward(ch, s, y_up)
        forward(ch, s, y_down)
        forward(ch, s, sibling)

    def own_rows(ch, d):
        if d:
            s = slot(plane_of(d), y, k)
            landed(ch, s)
            spread(ch, s)

    def near_rows(ch, d):
        turn = (k + d) % 2
        first = slot(plane_of(d), (y + NY - 1 + 2 * turn) % NY, k)
        second = slot(plane_of(d), (y + 1 + 2 * turn) % NY, k)
        landed(ch, first)
        forward(ch, first, device(x, zh, zl, (y + 1 + 2 * turn) % NY, k))
        forward(ch, first, sibling)
        landed(ch, second)
        forward(ch, second, sibling)

    def far_rows(ch, d):
        far = slot(plane_of(d), (y + 2) % NY, k)
        landed(ch, far)
        forward(ch, far, sibling)

    def product(ch, base, q):
        left = jnp.concatenate([gathered[ch][base + j] for j in range(2 * NY)], axis=1)
        right = jnp.concatenate(
            [
                jnp.concatenate([tiles[inv[0, (base + j) * 8 + 2 * q + h]] for h in range(2)], axis=1)
                for j in range(2 * NY)
            ],
            axis=0,
        )
        return jnp.dot(left, right, preferred_element_type=F32)

    def multiply(ch, d):
        for yy in range(NY):
            landed(ch, slot(plane_of(d), yy, 1 - k))
        base = slot(plane_of(d), 0, 0)
        if d < NZL - 1:

            def one(q, carry):
                value = product(ch, base, q)
                acc[ch][q] = value if d == 0 else acc[ch][q] + value
                return carry

            lax.fori_loop(0, NX, one, 0)
            return
        for j in range(NX):
            q = (x + 1 + j) % NX
            value = acc[ch][q] + product(ch, base, q)
            if j < NX - 1:
                part[ch][j] = value.astype(BF16)
                dev = device(q, zh, zl, y, k)
                send(part[ch].at[j], from_x[ch].at[j], rx_send.at[ch, j], rx_recv.at[ch, j], dev)
            else:
                acc[ch][q] = value

    def x_sum(ch, which):
        lanes = pl.ds(pl.multiple_of(which * 128, 128), 128)
        total = acc[ch][x, :, lanes]
        for j in range(NX - 1):
            total = total + from_x[ch][j, :, lanes].astype(F32)
        return total

    def over_x(ch):
        for j in range(NX - 1):
            arrived(from_x[ch].at[j], rx_send.at[ch, j], rx_recv.at[ch, j])
        to_z[ch][...] = x_sum(ch, 1 - zh).astype(BF16)
        send(to_z[ch], from_z[ch], rz_send.at[ch], rz_recv.at[ch], device(x, 1 - zh, zl, y, k))

    def over_z(ch):
        total = x_sum(ch, zh)
        arrived(from_z[ch], rz_send.at[ch], rz_recv.at[ch])
        rows = pl.ds(START[ch], WIDTH[ch])
        agg[SIDE[ch], rows] = (total + from_z[ch][...].astype(F32)).astype(BF16)

    def local(u):
        rows = UNIT_ROWS[u] // 2

        def share_of(core):
            start = pl.multiple_of(core * rows, rows)
            if u == 0:
                left = jnp.maximum(pre_t[pl.ds(start, rows)], jnp.zeros((), BF16))
                right = agg[0]
            else:
                left = agg[1, pl.ds(UNIT_START[u] - 512 + start, rows)]
                right = grad_t[...]
            return lax.dot_general(left, right, NT, preferred_element_type=F32)

        given[u][...] = share_of(1 - k).astype(BF16)
        send(given[u], core_in[u], core_send.at[u], core_recv.at[u], sibling)
        kept[u][...] = share_of(k)
        if u == 0:
            hidden = jnp.dot(weight[...], agg[0], preferred_element_type=F32)
            grad_t[...] = jnp.where(pre_t[...] > 0, hidden, 0.0).astype(BF16)

    def core_sum(u):
        arrived(core_in[u], core_send.at[u], core_recv.at[u])
        total = (kept[u][...] + core_in[u][...].astype(F32)).astype(BF16)
        wide = UNIT_ROWS[u]
        cuts = 512 // wide
        for m in range(NX * NY):
            top, left = (m // cuts) * 16, (m % cuts) * wide
            piece[u][m] = total[top : top + 16, left : left + wide]
        for m, dev in plane:
            send(piece[u].at[m], plane_in[u].at[me], plane_send.at[u, m], plane_recv.at[u, me], dev)

    def plane_sum(u):
        total = piece[u][me].astype(F32)
        for m, _ in plane:
            arrived(plane_in[u].at[m], plane_send.at[u, m], plane_recv.at[u, m])
            total = total + plane_in[u][m].astype(F32)
        z_in[u][z] = total.astype(BF16)
        for zz, dev in z_line:
            send(z_in[u].at[z], z_in[u].at[z], z_send.at[u, zz], z_recv.at[u, z], dev)

    def z_sum(u):
        for zz, _ in z_line:
            arrived(z_in[u].at[zz], z_send.at[u, zz], z_recv.at[u, zz])
        total = z_in[u][0].astype(F32)
        for zz in range(1, NZH * NZL):
            total = total + z_in[u][zz].astype(F32)
        final[u][k, me] = total.astype(BF16)
        ref = final[u].at[k, me]
        for m, dev in plane:
            send(ref, ref, fin_send.at[u, m], fin_recv.at[u, me], dev)

    def share(u):
        for m, _ in plane:
            arrived(final[u].at[k, m], fin_send.at[u, m], fin_recv.at[u, m])
        ref = final[u].at[k]
        send(ref, ref, last_send.at[u], last_recv.at[u], sibling)

    def finish(u):
        arrived(final[u].at[1 - k], last_send.at[u], last_recv.at[u])
        wide = UNIT_ROWS[u]
        cuts = 512 // wide
        base = UNIT_START[u]
        for core in range(2):
            for m in range(NX * NY):
                top, left = base + core * (wide // 2) + (m // cuts) * 16, (m % cuts) * wide
                out[top : top + 16, left : left + wide] = final[u][core, m]

    for ch in range(CHUNKS):
        for d in range(NZL - 1, 0, -1):
            forward(ch, c, device(x, zh, (zl + d) % NZL, y, k))
    for ch in range(CHUNKS):
        spread(ch, c)
    load_tiles.wait()

    steps = [(ch, d) for ch in range(CHUNKS) for d in range(NZL)]
    for i in range(len(steps) + 7):
        for lag, job in ((0, own_rows), (3, near_rows), (6, far_rows)):
            if 0 <= i - lag < len(steps):
                job(*steps[i - lag])
        if i == 17:
            over_x(0)
        if i == 21:
            over_x(1)
            over_z(0)
        if i >= 7:
            multiply(*steps[i - 7])
    over_x(2)
    over_z(1)
    local(0)
    over_x(3)
    core_sum(0)
    over_x(4)
    over_z(2)
    local(1)
    plane_sum(0)
    core_sum(1)
    over_z(3)
    over_z(4)
    local(2)
    z_sum(0)
    core_sum(2)
    plane_sum(1)
    share(0)
    plane_sum(2)
    z_sum(1)
    finish(0)
    z_sum(2)
    share(1)
    finish(1)
    share(2)
    finish(2)
    for copy in sends:
        copy.wait_send()


def shards(adj_tiles, tile_row, tile_col, tile_count, node_feats, pre_act, out_grad, second_weight):
    tiles = adj_tiles[0, 0]
    slots = tiles.shape[0]
    vmem = pltpu.VMEM
    dma = pltpu.SemaphoreType.DMA
    smem = pl.BlockSpec(memory_space=pltpu.SMEM)
    hbm = pl.BlockSpec(memory_space=pl.ANY)
    result = pl.pallas_call(
        whole_kernel,
        out_shape=jax.ShapeDtypeStruct((1024, 512), BF16),
        in_specs=[hbm, hbm, smem] + [hbm] * 5,
        out_specs=pl.BlockSpec(memory_space=pltpu.VMEM),
        scratch_shapes=[
            vmem((slots + 1, 128, 128), BF16),
            vmem((128, 512), BF16),
            vmem((128, 512), BF16),
            vmem((128, 512), BF16),
            vmem((512, 512), BF16),
            vmem((2, 1, slots), jnp.int32),
            vmem((8, 256), jnp.int32),
            pltpu.SMEM((8, 256), jnp.int32),
        ]
        + [vmem((32, n, 128), BF16) for n in WIDTH]
        + [vmem((NX, n, 256), F32) for n in WIDTH]
        + [vmem((3, n, 256), BF16) for n in WIDTH]
        + [vmem((3, n, 256), BF16) for n in WIDTH]
        + [vmem((n, 128), BF16) for n in WIDTH]
        + [vmem((n, 128), BF16) for n in WIDTH]
        + [vmem((2, 512, 128), BF16), vmem((512, 128), BF16), vmem((512, 128), BF16)]
        + [vmem((8, 16, n), BF16) for n in UNIT_ROWS]
        + [vmem((n // 2, 512), F32) for n in UNIT_ROWS]
        + [vmem((n // 2, 512), BF16) for n in UNIT_ROWS]
        + [vmem((n // 2, 512), BF16) for n in UNIT_ROWS]
        + [vmem((16, 16, n), BF16) for n in UNIT_ROWS]
        + [vmem((16, 16, n), BF16) for n in UNIT_ROWS]
        + [vmem((2, 16, 16, n), BF16) for n in UNIT_ROWS]
        + [
            dma((2,)),
            dma((6,)),
            dma((CHUNKS, 31)),
            dma((CHUNKS, 32)),
            dma((CHUNKS, 3)),
            dma((CHUNKS, 3)),
            dma((CHUNKS,)),
            dma((CHUNKS,)),
            dma((UNITS,)),
            dma((UNITS,)),
            dma((UNITS, 16)),
            dma((UNITS, 16)),
            dma((UNITS, 8)),
            dma((UNITS, 8)),
            dma((UNITS, 16)),
            dma((UNITS, 16)),
            dma((UNITS,)),
            dma((UNITS,)),
        ],
        compiler_params=pltpu.CompilerParams(
            collective_id=0, has_side_effects=True, vmem_limit_bytes=56 * 1024 * 1024
        ),
    )(tile_row[0], tile_col[0], tile_count, tiles, node_feats, pre_act, out_grad, second_weight)
    return result[512:].astype(F32), result[:512].astype(F32)


def solution(mesh):
    in_specs = (
        P("row", "col", None, None, None),
        P("row", "col", None),
        P("row", "col", None),
        P("row", "col"),
        P(("row", "col"), None),
        P(("col", "row"), None),
        P(("row", "col"), None),
        P(),
    )
    out_specs = (P(), P())
    return jax.shard_map(shards, mesh=mesh, in_specs=in_specs, out_specs=out_specs, check_vma=False)
```

```python
import functools

import jax
import jax.numpy as jnp
from jax import lax
from jax.experimental import pallas as pl
from jax.experimental.pallas import tpu as pltpu
from jax.sharding import PartitionSpec as P

MESH = pl.DeviceIdType.MESH
BF16 = jnp.bfloat16
F32 = jnp.float32
NX, NY, NZL, NZH = 4, 4, 4, 2
WIDTH = (256, 256, 256, 128, 128)
START = (0, 256, 0, 256, 384)
SIDE = (0, 0, 1, 1, 1)
CHUNKS = len(WIDTH)
UNIT_ROWS = (512, 256, 256)
UNIT_START = (0, 512, 768)
UNITS = len(UNIT_ROWS)
NT = (((1,), (1,)), ((), ()))


def whole_kernel(row_hbm, col_hbm, live, tiles_hbm, feats_hbm, pre_hbm, cot_hbm, weight_hbm, out, *scratch):
    scratch = list(scratch)

    def take(n=None):
        if n is None:
            return scratch.pop(0)
        return [scratch.pop(0) for _ in range(n)]

    tiles, feats, pre, cot, weight, places, table, inv = take(8)
    gathered, acc, part, from_x, to_z, from_z = (take(CHUNKS) for _ in range(6))
    agg, pre_t, grad_t = take(3)
    z_in, kept, given, core_in, piece, plane_in, final = (take(UNITS) for _ in range(7))
    tile_sem, load_sem, ag_send, ag_recv, rx_send, rx_recv, rz_send, rz_recv = take(8)
    core_send, core_recv, plane_send, plane_recv, z_send, z_recv = take(6)
    fin_send, fin_recv, last_send, last_recv = take(4)
    r = lax.axis_index("row")
    c = lax.axis_index("col")
    x, zh = r // NZH, r % NZH
    zl, y, k = c // (2 * NY), (c // 2) % NY, c % 2
    z = zh * NZL + zl
    live_slots = tiles_hbm.shape[0]

    def device(x_, zh_, zl_, y_, k_):
        return (x_ * NZH + zh_, (zl_ * NY + y_) * 2 + k_)

    def slot(zl_, y_, k_):
        return (zl_ * NY + y_) * 2 + k_

    sibling = device(x, zh, zl, y, 1 - k)
    y_up = device(x, zh, zl, (y + 1) % NY, k)
    y_down = device(x, zh, zl, (y + NY - 1) % NY, k)
    plane = []
    around = [(dx, dy) for dx in range(NX) for dy in range(NY) if dx or dy]
    for dx, dy in sorted(around, key=lambda p: -min(p[0], NX - p[0]) - min(p[1], NY - p[1])):
        xx, yy = (x + dx) % NX, (y + dy) % NY
        plane.append((xx * NY + yy, device(xx, zh, zl, yy, k)))
    z_line = []
    for dz in sorted(range(1, NZH * NZL), key=lambda n: -min(n, NZH * NZL - n)):
        zz = (z + dz) % (NZH * NZL)
        z_line.append((zz, device(x, zz // NZL, zz % NZL, y, k)))
    me = x * NY + y

    sends = []

    def send(src, dst, ssem, rsem, dev):
        copy = pltpu.make_async_remote_copy(
            src_ref=src, dst_ref=dst, send_sem=ssem, recv_sem=rsem, device_id=dev, device_id_type=MESH
        )
        copy.start()
        sends.append(copy)

    def arrived(ref, ssem, rsem):
        pltpu.make_async_remote_copy(
            src_ref=ref, dst_ref=ref, send_sem=ssem, recv_sem=rsem, device_id=sibling, device_id_type=MESH
        ).wait_recv()

    load_tiles = pltpu.make_async_copy(tiles_hbm, tiles.at[pl.ds(0, live_slots)], tile_sem.at[0])
    loads = [
        pltpu.make_async_copy(src, dst, load_sem.at[n])
        for n, (src, dst) in enumerate(
            [
                (cot_hbm, cot),
                (feats_hbm, feats),
                (row_hbm, places.at[0]),
                (col_hbm, places.at[1]),
                (pre_hbm, pre),
                (weight_hbm, weight),
            ]
        )
    ]
    for copy in loads:
        copy.start()
    load_tiles.start()

    barrier = pltpu.get_barrier_semaphore()
    greet = [d for _, d in z_line] + [d for _, d in plane] + [sibling]
    for dev in greet:
        pl.semaphore_signal(barrier, inc=1, device_id=dev, device_id_type=MESH)
    for side, source in enumerate((cot, feats)):
        loads[side].wait()
        turned = source[...].T
        for ch in range(CHUNKS):
            if SIDE[ch] == side:
                gathered[ch][c] = turned[START[ch] : START[ch] + WIDTH[ch]]
    loads[2].wait()
    loads[3].wait()
    turn = lax.broadcasted_iota(jnp.int32, (1, live_slots), 1)
    place = jnp.where(turn < live[0, 0], places[0] * 8 + places[1], -1)
    hit = place == lax.broadcasted_iota(jnp.int32, (256, live_slots), 0)
    found = jnp.min(jnp.where(hit, turn, live_slots), axis=1, keepdims=True)
    table[...] = jnp.broadcast_to(found, (256, 128)).T[0:8]
    to_scalar = pltpu.make_async_copy(table, inv, tile_sem.at[1])
    to_scalar.start()
    tiles[live_slots] = jnp.zeros(tiles.shape[1:], BF16)
    loads[4].wait()
    pre_t[...] = pre[...].T
    loads[5].wait()
    to_scalar.wait()
    pl.semaphore_wait(barrier, len(greet))

    counts = [0] * CHUNKS

    def forward(ch, s, dev):
        n = counts[ch]
        counts[ch] += 1
        ref = gathered[ch].at[s]
        send(ref, ref, ag_send.at[ch, n], ag_recv.at[ch, s], dev)

    def landed(ch, s):
        arrived(gathered[ch].at[s], ag_send.at[ch, 0], ag_recv.at[ch, s])

    def plane_of(d):
        return (zl + d) % NZL

    def spread(ch, s):
        forward(ch, s, y_up)
        forward(ch, s, y_down)
        forward(ch, s, sibling)

    def own_rows(ch, d):
        if d:
            s = slot(plane_of(d), y, k)
            landed(ch, s)
            spread(ch, s)

    def near_rows(ch, d):
        turn = (k + d) % 2
        first = slot(plane_of(d), (y + NY - 1 + 2 * turn) % NY, k)
        second = slot(plane_of(d), (y + 1 + 2 * turn) % NY, k)
        landed(ch, first)
        forward(ch, first, device(x, zh, zl, (y + 1 + 2 * turn) % NY, k))
        forward(ch, first, sibling)
        landed(ch, second)
        forward(ch, second, sibling)

    def far_rows(ch, d):
        far = slot(plane_of(d), (y + 2) % NY, k)
        landed(ch, far)
        forward(ch, far, sibling)

    def product(ch, base, q):
        left = jnp.concatenate([gathered[ch][base + j] for j in range(2 * NY)], axis=1)
        right = jnp.concatenate(
            [
                jnp.concatenate([tiles[inv[0, (base + j) * 8 + 2 * q + h]] for h in range(2)], axis=1)
                for j in range(2 * NY)
            ],
            axis=0,
        )
        return jnp.dot(left, right, preferred_element_type=F32)

    def multiply(ch, d):
        for yy in range(NY):
            landed(ch, slot(plane_of(d), yy, 1 - k))
        base = slot(plane_of(d), 0, 0)
        if d < NZL - 1:

            def one(q, carry):
                value = product(ch, base, q)
                acc[ch][q] = value if d == 0 else acc[ch][q] + value
                return carry

            lax.fori_loop(0, NX, one, 0)
            return
        for j in range(NX):
            q = (x + 1 + j) % NX
            value = acc[ch][q] + product(ch, base, q)
            if j < NX - 1:
                part[ch][j] = value.astype(BF16)
                dev = device(q, zh, zl, y, k)
                send(part[ch].at[j], from_x[ch].at[j], rx_send.at[ch, j], rx_recv.at[ch, j], dev)
            else:
                acc[ch][q] = value

    def x_sum(ch, which):
        lanes = pl.ds(pl.multiple_of(which * 128, 128), 128)
        total = acc[ch][x, :, lanes]
        for j in range(NX - 1):
            total = total + from_x[ch][j, :, lanes].astype(F32)
        return total

    def over_x(ch):
        for j in range(NX - 1):
            arrived(from_x[ch].at[j], rx_send.at[ch, j], rx_recv.at[ch, j])
        to_z[ch][...] = x_sum(ch, 1 - zh).astype(BF16)
        send(to_z[ch], from_z[ch], rz_send.at[ch], rz_recv.at[ch], device(x, 1 - zh, zl, y, k))

    def over_z(ch):
        total = x_sum(ch, zh)
        arrived(from_z[ch], rz_send.at[ch], rz_recv.at[ch])
        rows = pl.ds(START[ch], WIDTH[ch])
        agg[SIDE[ch], rows] = (total + from_z[ch][...].astype(F32)).astype(BF16)

    def local(u):
        rows = UNIT_ROWS[u] // 2

        def share_of(core):
            start = pl.multiple_of(core * rows, rows)
            if u == 0:
                left = jnp.maximum(pre_t[pl.ds(start, rows)], jnp.zeros((), BF16))
                right = agg[0]
            else:
                left = agg[1, pl.ds(UNIT_START[u] - 512 + start, rows)]
                right = grad_t[...]
            return lax.dot_general(left, right, NT, preferred_element_type=F32)

        given[u][...] = share_of(1 - k).astype(BF16)
        send(given[u], core_in[u], core_send.at[u], core_recv.at[u], sibling)
        kept[u][...] = share_of(k)
        if u == 0:
            hidden = jnp.dot(weight[...], agg[0], preferred_element_type=F32)
            grad_t[...] = jnp.where(pre_t[...] > 0, hidden, 0.0).astype(BF16)

    def core_sum(u):
        arrived(core_in[u], core_send.at[u], core_recv.at[u])
        total = (kept[u][...] + core_in[u][...].astype(F32)).astype(BF16)
        wide = UNIT_ROWS[u]
        cuts = 512 // wide
        for m in range(NX * NY):
            top, left = (m // cuts) * 16, (m % cuts) * wide
            piece[u][m] = total[top : top + 16, left : left + wide]
        for m, dev in plane:
            send(piece[u].at[m], plane_in[u].at[me], plane_send.at[u, m], plane_recv.at[u, me], dev)

    def plane_sum(u):
        total = piece[u][me].astype(F32)
        for m, _ in reversed(plane):
            arrived(plane_in[u].at[m], plane_send.at[u, m], plane_recv.at[u, m])
            total = total + plane_in[u][m].astype(F32)
        z_in[u][z] = total.astype(BF16)
        for zz, dev in z_line:
            send(z_in[u].at[z], z_in[u].at[z], z_send.at[u, zz], z_recv.at[u, z], dev)

    def z_sum(u):
        for zz, _ in z_line:
            arrived(z_in[u].at[zz], z_send.at[u, zz], z_recv.at[u, zz])
        total = z_in[u][0].astype(F32)
        for zz in range(1, NZH * NZL):
            total = total + z_in[u][zz].astype(F32)
        final[u][k, me] = total.astype(BF16)
        ref = final[u].at[k, me]
        for m, dev in plane:
            send(ref, ref, fin_send.at[u, m], fin_recv.at[u, me], dev)

    def share(u):
        for m, _ in plane:
            arrived(final[u].at[k, m], fin_send.at[u, m], fin_recv.at[u, m])
        ref = final[u].at[k]
        send(ref, ref, last_send.at[u], last_recv.at[u], sibling)

    def finish(u):
        arrived(final[u].at[1 - k], last_send.at[u], last_recv.at[u])
        wide = UNIT_ROWS[u]
        cuts = 512 // wide
        base = UNIT_START[u]
        for core in range(2):
            for m in range(NX * NY):
                top, left = base + core * (wide // 2) + (m // cuts) * 16, (m % cuts) * wide
                out[top : top + 16, left : left + wide] = final[u][core, m]

    for ch in range(CHUNKS):
        for d in range(NZL - 1, 0, -1):
            forward(ch, c, device(x, zh, (zl + d) % NZL, y, k))
    for ch in range(CHUNKS):
        spread(ch, c)
    load_tiles.wait()

    steps = [(ch, d) for ch in range(CHUNKS) for d in range(NZL)]
    for i in range(len(steps) + 9):
        for lag, job in ((0, own_rows), (4, near_rows), (8, far_rows)):
            if 0 <= i - lag < len(steps):
                job(*steps[i - lag])
        if i == 19:
            over_x(0)
        if i == 23:
            over_x(1)
            over_z(0)
        if i >= 9:
            multiply(*steps[i - 9])
    over_x(2)
    over_z(1)
    local(0)
    over_x(3)
    core_sum(0)
    over_x(4)
    over_z(2)
    local(1)
    plane_sum(0)
    core_sum(1)
    over_z(3)
    over_z(4)
    local(2)
    z_sum(0)
    core_sum(2)
    plane_sum(1)
    share(0)
    plane_sum(2)
    z_sum(1)
    finish(0)
    z_sum(2)
    share(1)
    finish(1)
    share(2)
    finish(2)
    for copy in sends:
        copy.wait_send()


def shards(adj_tiles, tile_row, tile_col, tile_count, node_feats, pre_act, out_grad, second_weight):
    tiles = adj_tiles[0, 0]
    slots = tiles.shape[0]
    vmem = pltpu.VMEM
    dma = pltpu.SemaphoreType.DMA
    smem = pl.BlockSpec(memory_space=pltpu.SMEM)
    hbm = pl.BlockSpec(memory_space=pl.ANY)
    result = pl.pallas_call(
        whole_kernel,
        out_shape=jax.ShapeDtypeStruct((1024, 512), BF16),
        in_specs=[hbm, hbm, smem] + [hbm] * 5,
        out_specs=pl.BlockSpec(memory_space=pltpu.VMEM),
        scratch_shapes=[
            vmem((slots + 1, 128, 128), BF16),
            vmem((128, 512), BF16),
            vmem((128, 512), BF16),
            vmem((128, 512), BF16),
            vmem((512, 512), BF16),
            vmem((2, 1, slots), jnp.int32),
            vmem((8, 256), jnp.int32),
            pltpu.SMEM((8, 256), jnp.int32),
        ]
        + [vmem((32, n, 128), BF16) for n in WIDTH]
        + [vmem((NX, n, 256), F32) for n in WIDTH]
        + [vmem((3, n, 256), BF16) for n in WIDTH]
        + [vmem((3, n, 256), BF16) for n in WIDTH]
        + [vmem((n, 128), BF16) for n in WIDTH]
        + [vmem((n, 128), BF16) for n in WIDTH]
        + [vmem((2, 512, 128), BF16), vmem((512, 128), BF16), vmem((512, 128), BF16)]
        + [vmem((8, 16, n), BF16) for n in UNIT_ROWS]
        + [vmem((n // 2, 512), F32) for n in UNIT_ROWS]
        + [vmem((n // 2, 512), BF16) for n in UNIT_ROWS]
        + [vmem((n // 2, 512), BF16) for n in UNIT_ROWS]
        + [vmem((16, 16, n), BF16) for n in UNIT_ROWS]
        + [vmem((16, 16, n), BF16) for n in UNIT_ROWS]
        + [vmem((2, 16, 16, n), BF16) for n in UNIT_ROWS]
        + [
            dma((2,)),
            dma((6,)),
            dma((CHUNKS, 31)),
            dma((CHUNKS, 32)),
            dma((CHUNKS, 3)),
            dma((CHUNKS, 3)),
            dma((CHUNKS,)),
            dma((CHUNKS,)),
            dma((UNITS,)),
            dma((UNITS,)),
            dma((UNITS, 16)),
            dma((UNITS, 16)),
            dma((UNITS, 8)),
            dma((UNITS, 8)),
            dma((UNITS, 16)),
            dma((UNITS, 16)),
            dma((UNITS,)),
            dma((UNITS,)),
        ],
        compiler_params=pltpu.CompilerParams(
            collective_id=0, has_side_effects=True, vmem_limit_bytes=56 * 1024 * 1024
        ),
    )(tile_row[0], tile_col[0], tile_count, tiles, node_feats, pre_act, out_grad, second_weight)
    return result[512:].astype(F32), result[:512].astype(F32)


def solution(mesh):
    in_specs = (
        P("row", "col", None, None, None),
        P("row", "col", None),
        P("row", "col", None),
        P("row", "col"),
        P(("row", "col"), None),
        P(("col", "row"), None),
        P(("row", "col"), None),
        P(),
    )
    out_specs = (P(), P())
    return jax.shard_map(shards, mesh=mesh, in_specs=in_specs, out_specs=out_specs, check_vma=False)
```

```python
import functools

import jax
import jax.numpy as jnp
from jax import lax
from jax.experimental import pallas as pl
from jax.experimental.pallas import tpu as pltpu
from jax.sharding import PartitionSpec as P

MESH = pl.DeviceIdType.MESH
BF16 = jnp.bfloat16
F32 = jnp.float32
NX, NY, NZL, NZH = 4, 4, 4, 2
WIDTH = (256, 256, 256, 128, 128)
START = (0, 256, 0, 256, 384)
SIDE = (0, 0, 1, 1, 1)
CHUNKS = len(WIDTH)
UNIT_ROWS = (512, 256, 256)
UNIT_START = (0, 512, 768)
UNITS = len(UNIT_ROWS)
NT = (((1,), (1,)), ((), ()))


def whole_kernel(row_hbm, col_hbm, live, tiles_hbm, feats_hbm, pre_hbm, cot_hbm, weight_hbm, out, *scratch):
    scratch = list(scratch)

    def take(n=None):
        if n is None:
            return scratch.pop(0)
        return [scratch.pop(0) for _ in range(n)]

    tiles, feats, pre, cot, weight, places, table, inv = take(8)
    gathered, acc, part, from_x, to_z, from_z = (take(CHUNKS) for _ in range(6))
    agg, pre_t, grad_t = take(3)
    z_in, kept, given, core_in, piece, plane_in, final = (take(UNITS) for _ in range(7))
    tile_sem, load_sem, ag_send, ag_recv, rx_send, rx_recv, rz_send, rz_recv = take(8)
    core_send, core_recv, plane_send, plane_recv, z_send, z_recv = take(6)
    fin_send, fin_recv, last_send, last_recv = take(4)
    r = lax.axis_index("row")
    c = lax.axis_index("col")
    x, zh = r // NZH, r % NZH
    zl, y, k = c // (2 * NY), (c // 2) % NY, c % 2
    z = zh * NZL + zl
    live_slots = tiles_hbm.shape[0]

    def device(x_, zh_, zl_, y_, k_):
        return (x_ * NZH + zh_, (zl_ * NY + y_) * 2 + k_)

    def slot(zl_, y_, k_):
        return (zl_ * NY + y_) * 2 + k_

    sibling = device(x, zh, zl, y, 1 - k)
    y_up = device(x, zh, zl, (y + 1) % NY, k)
    y_down = device(x, zh, zl, (y + NY - 1) % NY, k)
    plane = []
    around = [(dx, dy) for dx in range(NX) for dy in range(NY) if dx or dy]
    for dx, dy in sorted(around, key=lambda p: -min(p[0], NX - p[0]) - min(p[1], NY - p[1])):
        xx, yy = (x + dx) % NX, (y + dy) % NY
        plane.append((xx * NY + yy, device(xx, zh, zl, yy, k)))
    z_line = []
    for dz in sorted(range(1, NZH * NZL), key=lambda n: -min(n, NZH * NZL - n)):
        zz = (z + dz) % (NZH * NZL)
        z_line.append((zz, device(x, zz // NZL, zz % NZL, y, k)))
    me = x * NY + y

    sends = []

    def send(src, dst, ssem, rsem, dev):
        copy = pltpu.make_async_remote_copy(
            src_ref=src, dst_ref=dst, send_sem=ssem, recv_sem=rsem, device_id=dev, device_id_type=MESH
        )
        copy.start()
        sends.append(copy)

    def arrived(ref, ssem, rsem):
        pltpu.make_async_remote_copy(
            src_ref=ref, dst_ref=ref, send_sem=ssem, recv_sem=rsem, device_id=sibling, device_id_type=MESH
        ).wait_recv()

    load_tiles = pltpu.make_async_copy(tiles_hbm, tiles.at[pl.ds(0, live_slots)], tile_sem.at[0])
    loads = [
        pltpu.make_async_copy(src, dst, load_sem.at[n])
        for n, (src, dst) in enumerate(
            [
                (cot_hbm, cot),
                (feats_hbm, feats),
                (row_hbm, places.at[0]),
                (col_hbm, places.at[1]),
                (pre_hbm, pre),
                (weight_hbm, weight),
            ]
        )
    ]
    for copy in loads:
        copy.start()
    load_tiles.start()

    barrier = pltpu.get_barrier_semaphore()
    greet = [d for _, d in z_line] + [d for _, d in plane] + [sibling]
    for dev in greet:
        pl.semaphore_signal(barrier, inc=1, device_id=dev, device_id_type=MESH)
    for side, source in enumerate((cot, feats)):
        loads[side].wait()
        turned = source[...].T
        for ch in range(CHUNKS):
            if SIDE[ch] == side:
                gathered[ch][c] = turned[START[ch] : START[ch] + WIDTH[ch]]
    loads[2].wait()
    loads[3].wait()
    turn = lax.broadcasted_iota(jnp.int32, (1, live_slots), 1)
    place = jnp.where(turn < live[0, 0], places[0] * 8 + places[1], -1)
    hit = place == lax.broadcasted_iota(jnp.int32, (256, live_slots), 0)
    found = jnp.min(jnp.where(hit, turn, live_slots), axis=1, keepdims=True)
    table[...] = jnp.broadcast_to(found, (256, 128)).T[0:8]
    to_scalar = pltpu.make_async_copy(table, inv, tile_sem.at[1])
    to_scalar.start()
    tiles[live_slots] = jnp.zeros(tiles.shape[1:], BF16)
    loads[4].wait()
    pre_t[...] = pre[...].T
    loads[5].wait()
    to_scalar.wait()
    pl.semaphore_wait(barrier, len(greet))

    counts = [0] * CHUNKS

    def forward(ch, s, dev):
        n = counts[ch]
        counts[ch] += 1
        ref = gathered[ch].at[s]
        send(ref, ref, ag_send.at[ch, n], ag_recv.at[ch, s], dev)

    def landed(ch, s):
        arrived(gathered[ch].at[s], ag_send.at[ch, 0], ag_recv.at[ch, s])

    def plane_of(d):
        return (zl + d) % NZL

    def spread(ch, s):
        forward(ch, s, y_up)
        forward(ch, s, y_down)
        forward(ch, s, sibling)

    def own_rows(ch, d):
        if d:
            s = slot(plane_of(d), y, k)
            landed(ch, s)
            spread(ch, s)

    def near_rows(ch, d):
        turn = (k + d) % 2
        first = slot(plane_of(d), (y + NY - 1 + 2 * turn) % NY, k)
        second = slot(plane_of(d), (y + 1 + 2 * turn) % NY, k)
        landed(ch, first)
        forward(ch, first, device(x, zh, zl, (y + 1 + 2 * turn) % NY, k))
        forward(ch, first, sibling)
        landed(ch, second)
        forward(ch, second, sibling)

    def far_rows(ch, d):
        far = slot(plane_of(d), (y + 2) % NY, k)
        landed(ch, far)
        forward(ch, far, sibling)

    def product(ch, base, q):
        left = jnp.concatenate([gathered[ch][base + j] for j in range(2 * NY)], axis=1)
        right = jnp.concatenate(
            [
                jnp.concatenate([tiles[inv[0, (base + j) * 8 + 2 * q + h]] for h in range(2)], axis=1)
                for j in range(2 * NY)
            ],
            axis=0,
        )
        return jnp.dot(left, right, preferred_element_type=F32)

    def multiply(ch, d):
        for yy in range(NY):
            landed(ch, slot(plane_of(d), yy, 1 - k))
        base = slot(plane_of(d), 0, 0)
        if d < NZL - 1:

            def one(q, carry):
                value = product(ch, base, q)
                acc[ch][q] = value if d == 0 else acc[ch][q] + value
                return carry

            lax.fori_loop(0, NX, one, 0)
            return
        for j in (1, 0, 2, 3):
            q = (x + 1 + j) % NX
            value = acc[ch][q] + product(ch, base, q)
            if j < NX - 1:
                part[ch][j] = value.astype(BF16)
                dev = device(q, zh, zl, y, k)
                send(part[ch].at[j], from_x[ch].at[j], rx_send.at[ch, j], rx_recv.at[ch, j], dev)
            else:
                acc[ch][q] = value

    def x_sum(ch, which):
        lanes = pl.ds(pl.multiple_of(which * 128, 128), 128)
        total = acc[ch][x, :, lanes]
        for j in range(NX - 1):
            total = total + from_x[ch][j, :, lanes].astype(F32)
        return total

    def over_x(ch):
        for j in range(NX - 1):
            arrived(from_x[ch].at[j], rx_send.at[ch, j], rx_recv.at[ch, j])
        to_z[ch][...] = x_sum(ch, 1 - zh).astype(BF16)
        send(to_z[ch], from_z[ch], rz_send.at[ch], rz_recv.at[ch], device(x, 1 - zh, zl, y, k))

    def over_z(ch):
        total = x_sum(ch, zh)
        arrived(from_z[ch], rz_send.at[ch], rz_recv.at[ch])
        rows = pl.ds(START[ch], WIDTH[ch])
        agg[SIDE[ch], rows] = (total + from_z[ch][...].astype(F32)).astype(BF16)

    def local(u):
        rows = UNIT_ROWS[u] // 2

        def share_of(core):
            start = pl.multiple_of(core * rows, rows)
            if u == 0:
                left = jnp.maximum(pre_t[pl.ds(start, rows)], jnp.zeros((), BF16))
                right = agg[0]
            else:
                left = agg[1, pl.ds(UNIT_START[u] - 512 + start, rows)]
                right = grad_t[...]
            return lax.dot_general(left, right, NT, preferred_element_type=F32)

        given[u][...] = share_of(1 - k).astype(BF16)
        send(given[u], core_in[u], core_send.at[u], core_recv.at[u], sibling)
        kept[u][...] = share_of(k)
        if u == 0:
            hidden = jnp.dot(weight[...], agg[0], preferred_element_type=F32)
            grad_t[...] = jnp.where(pre_t[...] > 0, hidden, 0.0).astype(BF16)

    def core_sum(u):
        arrived(core_in[u], core_send.at[u], core_recv.at[u])
        total = (kept[u][...] + core_in[u][...].astype(F32)).astype(BF16)
        wide = UNIT_ROWS[u]
        cuts = 512 // wide
        for m in range(NX * NY):
            top, left = (m // cuts) * 16, (m % cuts) * wide
            piece[u][m] = total[top : top + 16, left : left + wide]
        for m, dev in plane:
            send(piece[u].at[m], plane_in[u].at[me], plane_send.at[u, m], plane_recv.at[u, me], dev)

    def plane_sum(u):
        total = piece[u][me].astype(F32)
        for m, _ in reversed(plane):
            arrived(plane_in[u].at[m], plane_send.at[u, m], plane_recv.at[u, m])
            total = total + plane_in[u][m].astype(F32)
        z_in[u][z] = total.astype(BF16)
        for zz, dev in z_line:
            send(z_in[u].at[z], z_in[u].at[z], z_send.at[u, zz], z_recv.at[u, z], dev)

    def z_sum(u):
        for zz, _ in z_line:
            arrived(z_in[u].at[zz], z_send.at[u, zz], z_recv.at[u, zz])
        total = z_in[u][0].astype(F32)
        for zz in range(1, NZH * NZL):
            total = total + z_in[u][zz].astype(F32)
        final[u][k, me] = total.astype(BF16)
        ref = final[u].at[k, me]
        for m, dev in plane:
            send(ref, ref, fin_send.at[u, m], fin_recv.at[u, me], dev)

    def share(u):
        for m, _ in plane:
            arrived(final[u].at[k, m], fin_send.at[u, m], fin_recv.at[u, m])
        ref = final[u].at[k]
        send(ref, ref, last_send.at[u], last_recv.at[u], sibling)

    def finish(u):
        arrived(final[u].at[1 - k], last_send.at[u], last_recv.at[u])
        wide = UNIT_ROWS[u]
        cuts = 512 // wide
        base = UNIT_START[u]
        for core in range(2):
            for m in range(NX * NY):
                top, left = base + core * (wide // 2) + (m // cuts) * 16, (m % cuts) * wide
                out[top : top + 16, left : left + wide] = final[u][core, m]

    for ch in range(CHUNKS):
        for d in range(NZL - 1, 0, -1):
            forward(ch, c, device(x, zh, (zl + d) % NZL, y, k))
    for ch in range(CHUNKS):
        spread(ch, c)
    load_tiles.wait()

    steps = [(ch, d) for ch in range(CHUNKS) for d in range(NZL)]
    for i in range(len(steps) + 9):
        for lag, job in ((0, own_rows), (4, near_rows), (8, far_rows)):
            if 0 <= i - lag < len(steps):
                job(*steps[i - lag])
        if i == 19:
            over_x(0)
        if i == 23:
            over_x(1)
            over_z(0)
        if i >= 9:
            multiply(*steps[i - 9])
    over_x(2)
    over_z(1)
    local(0)
    over_x(3)
    core_sum(0)
    over_x(4)
    over_z(2)
    local(1)
    plane_sum(0)
    core_sum(1)
    over_z(3)
    over_z(4)
    local(2)
    z_sum(0)
    core_sum(2)
    plane_sum(1)
    share(0)
    plane_sum(2)
    z_sum(1)
    finish(0)
    z_sum(2)
    share(1)
    finish(1)
    share(2)
    finish(2)
    for copy in sends:
        copy.wait_send()


def shards(adj_tiles, tile_row, tile_col, tile_count, node_feats, pre_act, out_grad, second_weight):
    tiles = adj_tiles[0, 0]
    slots = tiles.shape[0]
    vmem = pltpu.VMEM
    dma = pltpu.SemaphoreType.DMA
    smem = pl.BlockSpec(memory_space=pltpu.SMEM)
    hbm = pl.BlockSpec(memory_space=pl.ANY)
    result = pl.pallas_call(
        whole_kernel,
        out_shape=jax.ShapeDtypeStruct((1024, 512), BF16),
        in_specs=[hbm, hbm, smem] + [hbm] * 5,
        out_specs=pl.BlockSpec(memory_space=pltpu.VMEM),
        scratch_shapes=[
            vmem((slots + 1, 128, 128), BF16),
            vmem((128, 512), BF16),
            vmem((128, 512), BF16),
            vmem((128, 512), BF16),
            vmem((512, 512), BF16),
            vmem((2, 1, slots), jnp.int32),
            vmem((8, 256), jnp.int32),
            pltpu.SMEM((8, 256), jnp.int32),
        ]
        + [vmem((32, n, 128), BF16) for n in WIDTH]
        + [vmem((NX, n, 256), F32) for n in WIDTH]
        + [vmem((3, n, 256), BF16) for n in WIDTH]
        + [vmem((3, n, 256), BF16) for n in WIDTH]
        + [vmem((n, 128), BF16) for n in WIDTH]
        + [vmem((n, 128), BF16) for n in WIDTH]
        + [vmem((2, 512, 128), BF16), vmem((512, 128), BF16), vmem((512, 128), BF16)]
        + [vmem((8, 16, n), BF16) for n in UNIT_ROWS]
        + [vmem((n // 2, 512), F32) for n in UNIT_ROWS]
        + [vmem((n // 2, 512), BF16) for n in UNIT_ROWS]
        + [vmem((n // 2, 512), BF16) for n in UNIT_ROWS]
        + [vmem((16, 16, n), BF16) for n in UNIT_ROWS]
        + [vmem((16, 16, n), BF16) for n in UNIT_ROWS]
        + [vmem((2, 16, 16, n), BF16) for n in UNIT_ROWS]
        + [
            dma((2,)),
            dma((6,)),
            dma((CHUNKS, 31)),
            dma((CHUNKS, 32)),
            dma((CHUNKS, 3)),
            dma((CHUNKS, 3)),
            dma((CHUNKS,)),
            dma((CHUNKS,)),
            dma((UNITS,)),
            dma((UNITS,)),
            dma((UNITS, 16)),
            dma((UNITS, 16)),
            dma((UNITS, 8)),
            dma((UNITS, 8)),
            dma((UNITS, 16)),
            dma((UNITS, 16)),
            dma((UNITS,)),
            dma((UNITS,)),
        ],
        compiler_params=pltpu.CompilerParams(
            collective_id=0, has_side_effects=True, vmem_limit_bytes=56 * 1024 * 1024
        ),
    )(tile_row[0], tile_col[0], tile_count, tiles, node_feats, pre_act, out_grad, second_weight)
    return result[512:].astype(F32), result[:512].astype(F32)


def solution(mesh):
    in_specs = (
        P("row", "col", None, None, None),
        P("row", "col", None),
        P("row", "col", None),
        P("row", "col"),
        P(("row", "col"), None),
        P(("col", "row"), None),
        P(("row", "col"), None),
        P(),
    )
    out_specs = (P(), P())
    return jax.shard_map(shards, mesh=mesh, in_specs=in_specs, out_specs=out_specs, check_vma=False)
```
